32 devices in a mesh: ctx: 8 (over z, core), heads: 4 (over y, x).
Axes of the slice: x: 2, y: 2, z: 4, core: 2. Of those that a mesh axis runs over, the one named last changes fastest.
Arguments:
- sharer_k: bfloat16 [8, 1024, 8192], P(None, 'ctx', 'heads'), may hold values from -6 to 6
- sharer_v: bfloat16 [8, 1024, 8192], P(None, 'ctx', 'heads'), may hold values from -6 to 6
- recv_k: bfloat16 [8, 1024, 8192], P('ctx', None, 'heads'), may hold values from -6 to 6
- recv_v: bfloat16 [8, 1024, 8192], P('ctx', None, 'heads'), may hold values from -6 to 6
- mixer_in: bfloat16 [4, 8192, 2, 512], P(None, 'heads'), may hold values from -0.03125 to 0.03125
- mixer_out: bfloat16 [2, 512, 8192], P(None, None, 'heads'), may hold values from -0.25 to 0.25
- mixer_gain: float32 [2, 64], P(None, 'heads'), may hold values from 0.5 to 2
- queries: bfloat16 [8, 256, 8192], P('ctx', None, 'heads'), may hold values from -40 to 40, as said below
- suffix_k: bfloat16 [8, 256, 8192], P('ctx', None, 'heads'), may hold values from -40 to 40, as said below
- suffix_v: bfloat16 [8, 256, 8192], P('ctx', None, 'heads'), may hold values from -6 to 6
- suffix_len: int32 [8], P('ctx'), may hold values from 64 to 256, as said below
- cache_offset: int32 [8], P('ctx'), may hold values from 512 to 1024, as said below
Outputs:
- attended: bfloat16 [8, 256, 8192], P('ctx', None, 'heads')
- merged_k: bfloat16 [8, 1024, 8192], P('ctx', None, 'heads')
- merged_v: bfloat16 [8, 1024, 8192], P('ctx', None, 'heads')
The draws below stay inside these ranges and needn't reach their ends.
Inputs may be any that keep to these rules, and one draw needn't show every extreme that they name: Values of queries lie within this range. Values of suffix_k lie within this range. `suffix_len`: some request has 256 live rows and some has 64. Suffix row i of request r stands at position cache_offset[r] + i; some request sees all 1024 cached positions and some sees 1024 // 2.
All inputs are finite; a program needn't handle non-finite values.
Results may differ from the reference program's by a relative error of at most 0.0093.
Values may be sent and summed in bfloat16 or wider, within the bound.
A program may use at most 192 MiB of HBM per device.

```python
import math
import jax
import jax.numpy as jnp
from jax import lax

H = 64
HD = 128
R = 512
SUF = 256
REQ = 8
CTX = 1024


def joint_rows(key):
    base = jax.random.fold_in(key, 7)
    keys = jax.random.split(base, 2)
    query_draw = jax.random.truncated_normal(keys[0], -6.0, 6.0, (REQ, SUF, H, HD), jnp.float32)
    key_draw = jax.random.truncated_normal(keys[1], -6.0, 6.0, (REQ, SUF, H, HD), jnp.float32)
    return (query_draw.reshape(REQ, SUF, H * HD), key_draw.reshape(REQ, SUF, H * HD))


def draw_queries(key, part):
    return joint_rows(key)[0].astype(jnp.bfloat16)


def draw_suffix_k(key, part):
    return joint_rows(key)[1].astype(jnp.bfloat16)


def draw_suffix_len(key, part):
    keys = jax.random.split(jax.random.fold_in(key, 11), 2)
    values = jax.random.randint(keys[0], (REQ,), SUF // 4, SUF + 1)
    order = jax.random.permutation(keys[1], REQ)
    values = values.at[order[0]].set(SUF).at[order[1]].set(SUF // 4)
    return values.astype(jnp.int32)


def draw_cache_offset(key, part):
    keys = jax.random.split(jax.random.fold_in(key, 13), 2)
    values = jax.random.randint(keys[0], (REQ,), CTX // 2, CTX + 1)
    order = jax.random.permutation(keys[1], REQ)
    values = values.at[order[0]].set(CTX).at[order[1]].set(CTX // 2)
    return values.astype(jnp.int32)


def steps_of(rng, extent, cuts, least, largest):
    def one(axis_at, parts):
        steps = jax.random.uniform(jax.random.fold_in(jax.random.fold_in(rng, 6), axis_at), (parts,), jnp.float32, least / len(cuts), largest / len(cuts))
        return jnp.repeat(jnp.exp(steps), extent[axis_at] // parts).reshape((-1,) + (1,) * (len(extent) - axis_at - 1))

    level = one(*cuts[0])
    for cut in cuts[1:]:
        level = level * one(*cut)
    return level


def scatter_about(key, extent, width, most, cuts=(), dtype=jnp.bfloat16):
    array = jax.random.normal(key, extent, jnp.float32) * width
    if len(cuts) > 0:
        array = steps_of(key, extent, cuts, -0.22, 0.18) * array
    return jnp.clip(array, min=-most, max=most).astype(dtype)


def setup_inputs(seed: int = 0) -> dict:
    seeds = jax.random.split(jax.random.key(seed), 13)
    sharer_k = scatter_about(seeds[0], (REQ, CTX, H * HD), 1.0, 6.0, ((1, 8), (2, 4)))
    sharer_v = scatter_about(seeds[1], (REQ, CTX, H * HD), 1.0, 6.0, ((1, 8), (2, 4)))
    recv_k = scatter_about(seeds[2], (REQ, CTX, H * HD), 1.0, 6.0, ((0, 8), (2, 4)))
    recv_v = scatter_about(seeds[3], (REQ, CTX, H * HD), 1.0, 6.0, ((0, 8), (2, 4)))
    mixer_in = scatter_about(seeds[4], (4, H * HD, 2, R), (4 * H * HD) ** -0.5, 0.03125, ((1, 4),))
    mixer_out = scatter_about(seeds[5], (2, R, H * HD), R ** -0.5, 0.25, ((2, 4),))
    mixer_gain = jnp.clip(jnp.exp(math.log(2.0) - 1.3862944 * jax.random.uniform(seeds[6], (2, H), jnp.float32) ** steps_of(seeds[6], (2, H), ((1, 4),), -0.2, 0.2)), 0.5, 2.0)
    queries = draw_queries(jax.random.fold_in(seeds[12], 71), 0)
    suffix_k = draw_suffix_k(jax.random.fold_in(seeds[12], 71), 0)
    suffix_v = scatter_about(seeds[9], (REQ, SUF, H * HD), 1.0, 6.0, ((0, 8), (2, 4)))
    suffix_len = draw_suffix_len(jax.random.fold_in(seeds[12], 71), 0)
    cache_offset = draw_cache_offset(jax.random.fold_in(seeds[12], 71), 0)
    return dict(sharer_k=sharer_k, sharer_v=sharer_v, recv_k=recv_k, recv_v=recv_v, mixer_in=mixer_in, mixer_out=mixer_out, mixer_gain=mixer_gain, queries=queries, suffix_k=suffix_k, suffix_v=suffix_v, suffix_len=suffix_len, cache_offset=cache_offset)


def merge_request(sharer_keys, sharer_vals, recv_keys, recv_vals, w_matrix, mixer_out, gain_rows):
    joined = jnp.concatenate([sharer_keys, sharer_vals, recv_keys, recv_vals], axis=1)
    pre = jnp.dot(joined, w_matrix, preferred_element_type=jnp.float32)
    hidden = (jax.nn.silu(pre[:, :R]) * pre[:, R:]).astype(jnp.bfloat16)
    delta_k = jnp.dot(hidden, mixer_out[0], preferred_element_type=jnp.float32)
    delta_v = jnp.dot(hidden, mixer_out[1], preferred_element_type=jnp.float32)
    merged_k = (recv_keys.astype(jnp.float32) + gain_rows[0] * delta_k).astype(jnp.bfloat16)
    merged_v = (recv_vals.astype(jnp.float32) + gain_rows[1] * delta_v).astype(jnp.bfloat16)
    return (merged_k, merged_v)

def attend(query_rows, merged_k, merged_v, own_keys, own_vals, length, offset):
    score_scale = 1.0 / math.sqrt(HD)
    query_heads = query_rows.astype(jnp.float32).reshape(SUF, H, HD)
    cache_keys = lax.optimization_barrier(merged_k).astype(jnp.float32).reshape(CTX, H, HD)
    cache_vals = lax.optimization_barrier(merged_v).astype(jnp.float32).reshape(CTX, H, HD)
    suffix_keys = own_keys.astype(jnp.float32).reshape(SUF, H, HD)
    suffix_vals = own_vals.astype(jnp.float32).reshape(SUF, H, HD)
    cache_scores = jnp.einsum('ihd,phd->hip', query_heads, cache_keys) * score_scale
    own_scores = jnp.einsum('ihd,jhd->hij', query_heads, suffix_keys) * score_scale
    cache_seen = jnp.arange(CTX)[None, None, :] < offset
    row_index = jnp.arange(SUF)
    own_seen = (row_index[None, :] <= row_index[:, None])[None, :, :]
    cache_scores = jnp.where(cache_seen, cache_scores, -jnp.inf)
    own_scores = jnp.where(own_seen, own_scores, -jnp.inf)
    row_peak = jnp.maximum(lax.optimization_barrier(jnp.max(cache_scores, axis=2)), lax.optimization_barrier(jnp.max(own_scores, axis=2)))[:, :, None]
    cache_numer = jnp.exp(cache_scores - row_peak)
    own_numer = jnp.exp(own_scores - row_peak)
    row_denom = lax.optimization_barrier(jnp.sum(cache_numer, axis=2)) + lax.optimization_barrier(jnp.sum(own_numer, axis=2))
    cache_probs = lax.optimization_barrier(cache_numer.astype(jnp.bfloat16)).astype(jnp.float32)
    own_probs = lax.optimization_barrier(own_numer.astype(jnp.bfloat16)).astype(jnp.float32)
    blended = jnp.einsum('hip,phd->ihd', cache_probs, cache_vals) + jnp.einsum('hij,jhd->ihd', own_probs, suffix_vals)
    blended = blended / jnp.transpose(row_denom)[:, :, None]
    alive_rows = (row_index < length)[:, None, None]
    return jnp.where(alive_rows, blended, 0.0).reshape(SUF, H * HD).astype(jnp.bfloat16)

def reference(sharer_k, sharer_v, recv_k, recv_v, mixer_in, mixer_out, mixer_gain, queries, suffix_k, suffix_v, suffix_len, cache_offset):
    w_matrix = mixer_in.reshape(4 * H * HD, 2 * R)
    gain_rows = jnp.repeat(mixer_gain, HD, axis=1)

    def one_request(bundle):
        sharer_keys, sharer_vals, recv_keys, recv_vals, query_rows, own_keys, own_vals, length, offset = bundle
        merged_k, merged_v = merge_request(sharer_keys, sharer_vals, recv_keys, recv_vals, w_matrix, mixer_out, gain_rows)
        attended = attend(query_rows, merged_k, merged_v, own_keys, own_vals, length, offset)
        return (attended, merged_k, merged_v)
    attended, merged_k, merged_v = lax.map(one_request, (sharer_k, sharer_v, recv_k, recv_v, queries, suffix_k, suffix_v, suffix_len, cache_offset))
    return (attended, merged_k, merged_v)
```

```python
import functools
import math

import jax
import jax.numpy as jnp
from jax import lax
from jax.experimental import pallas as pl
from jax.experimental.pallas import tpu as pltpu
from jax.sharding import PartitionSpec as P

HD = 128


def merge_attend_kernel(
    offset_ref,
    length_ref,
    gain_ref,
    hidden_ref,
    out_w_ref,
    recv_k_ref,
    recv_v_ref,
    q_ref,
    suf_k_ref,
    suf_v_ref,
    att_ref,
    mk_ref,
    mv_ref,
    *,
    heads,
    row_block,
):
    request = pl.program_id(0)
    group = pl.program_id(1)
    ctx_total = mk_ref.shape[1]
    query_rows = q_ref.shape[1]
    offset = offset_ref[request]
    length = length_ref[request]
    scale = 1.0 / math.sqrt(HD)
    for member, (recv_ref, merged_ref) in enumerate(((recv_k_ref, mk_ref), (recv_v_ref, mv_ref))):
        for start in range(0, ctx_total, row_block):
            rows = pl.ds(start, row_block)
            delta = jnp.dot(
                hidden_ref[0, rows, :], out_w_ref[member], preferred_element_type=jnp.float32
            )
            for head in range(heads):
                cols = slice(head * HD, (head + 1) * HD)
                gain = gain_ref[member, group * heads + head]
                merged_ref[0, rows, cols] = (
                    recv_ref[0, rows, cols].astype(jnp.float32) + gain * delta[:, cols]
                ).astype(jnp.bfloat16)
    half = ctx_total // 2
    late_pos = half + lax.broadcasted_iota(jnp.int32, (1, ctx_total - half), 1)
    late_seen = late_pos < offset
    own_seen = lax.broadcasted_iota(jnp.int32, (query_rows, query_rows), 1) <= (
        lax.broadcasted_iota(jnp.int32, (query_rows, query_rows), 0)
    )
    alive = lax.broadcasted_iota(jnp.int32, (query_rows, 1), 0) < length
    contract = (((1,), (1,)), ((), ()))
    for head in range(heads):
        cols = slice(head * HD, (head + 1) * HD)
        query = q_ref[0, :, cols]

        def scores_of(keys):
            return lax.dot_general(query, keys, contract, preferred_element_type=jnp.float32)

        early = scores_of(mk_ref[0, :half, cols])
        late = jnp.where(late_seen, scores_of(mk_ref[0, half:, cols]), -jnp.inf)
        own = jnp.where(own_seen, scores_of(suf_k_ref[0, :, cols]), -jnp.inf)
        peak = jnp.maximum(
            jnp.maximum(
                jnp.max(early, axis=1, keepdims=True), jnp.max(late, axis=1, keepdims=True)
            ),
            jnp.max(own, axis=1, keepdims=True),
        )
        denom = None
        blended = None
        for part, values in (
            (early, mv_ref[0, :half, cols]),
            (late, mv_ref[0, half:, cols]),
            (own, suf_v_ref[0, :, cols]),
        ):
            numer = jnp.exp((part - peak) * scale)
            total = jnp.sum(numer, axis=1, keepdims=True)
            mixed = jnp.dot(
                numer.astype(jnp.bfloat16), values, preferred_element_type=jnp.float32
            )
            denom = total if denom is None else denom + total
            blended = mixed if blended is None else blended + mixed
        att_ref[0, :, cols] = jnp.where(alive, blended / denom, 0.0).astype(jnp.bfloat16)


def merge_attend(
    hidden, mixer_out, mixer_gain, recv_k, recv_v, queries, suffix_k, suffix_v, suffix_len, cache_offset
):
    requests, ctx_total, width = recv_k.shape
    query_rows = queries.shape[1]
    rank = hidden.shape[-1]
    heads = 2
    lanes = heads * HD
    row_block = min(256, ctx_total)

    def by_head(rows):
        return pl.BlockSpec((1, rows, lanes), lambda r, g: (r, 0, g))

    smem = pl.BlockSpec(memory_space=pltpu.SMEM)
    return pl.pallas_call(
        functools.partial(merge_attend_kernel, heads=heads, row_block=row_block),
        grid=(requests, width // lanes),
        in_specs=[
            smem,
            smem,
            smem,
            pl.BlockSpec((1, ctx_total, rank), lambda r, g: (r, 0, 0)),
            pl.BlockSpec((2, rank, lanes), lambda r, g: (0, 0, g)),
            by_head(ctx_total),
            by_head(ctx_total),
            by_head(query_rows),
            by_head(query_rows),
            by_head(query_rows),
        ],
        out_specs=[by_head(query_rows), by_head(ctx_total), by_head(ctx_total)],
        out_shape=[
            jax.ShapeDtypeStruct(queries.shape, jnp.bfloat16),
            jax.ShapeDtypeStruct(recv_k.shape, jnp.bfloat16),
            jax.ShapeDtypeStruct(recv_v.shape, jnp.bfloat16),
        ],
        compiler_params=pltpu.CompilerParams(
            dimension_semantics=("arbitrary", "arbitrary"), vmem_limit_bytes=48 * 1024 * 1024
        ),
        name="merge_attend",
    )(
        cache_offset,
        suffix_len,
        mixer_gain,
        hidden,
        mixer_out,
        recv_k,
        recv_v,
        queries,
        suffix_k,
        suffix_v,
    )


def exchange_kernel(
    sharer_k_ref,
    sharer_v_ref,
    recv_k_ref,
    recv_v_ref,
    w_hbm,
    out_ref,
    x_ref,
    packed_ref,
    w_ref,
    part_ref,
    landed_ref,
    passed_ref,
    share_ref,
    moved_ref,
    hidden_ref,
    x_sem,
    w_sem,
    sum_send,
    sum_recv,
    move_send,
    move_recv,
    gather_send,
    gather_recv,
    out_sem,
    *,
    ctx_size,
    head_size,
    chunks,
):
    my_ctx = lax.axis_index("ctx")
    my_head = lax.axis_index("heads")
    group = ctx_size // chunks
    block_rows, width = x_ref.shape[2:]
    rank = w_ref.shape[-1]
    sub = block_rows // head_size
    w_rows = math.gcd(width, 128)
    square = head_size == 4
    flat_ref = packed_ref.reshape(4, 2 * width, rank)

    def ctx_of(shift):
        return lax.rem(my_ctx + shift + ctx_size, ctx_size)

    def head_of(shift):
        return lax.rem(my_head + shift, head_size)

    def x_copy(member, step):
        sharer = (sharer_k_ref, sharer_v_ref)[member]
        return pltpu.make_async_copy(
            sharer.at[ctx_of(1 + step)], x_ref.at[member, step], x_sem.at[member, step]
        )

    def y_copy(member, step):
        recv = (recv_k_ref, recv_v_ref)[member]
        return pltpu.make_async_copy(
            recv.at[ctx_of(-1 - step)],
            x_ref.at[member, ctx_size + step],
            x_sem.at[member, ctx_size + step],
        )

    def w_copy(slab):
        return pltpu.make_async_copy(w_hbm.at[slab], packed_ref.at[slab], w_sem.at[slab])

    def sum_copy(chunk, shift):
        target = head_of(shift)
        rows = pl.ds(chunk * group, group)
        return pltpu.make_async_remote_copy(
            src_ref=part_ref.at[rows, target],
            dst_ref=landed_ref.at[shift - 1, rows],
            send_sem=sum_send.at[chunk, shift - 1],
            recv_sem=sum_recv.at[chunk, shift - 1],
            device_id=(my_ctx, target),
            device_id_type=pl.DeviceIdType.MESH,
        )

    def pair_copy(chunk, stage, half):
        near = (my_head + 1 - 2 * lax.rem(my_head, 2), lax.rem(my_head + 2, 4))
        target, other = near[half], near[1 - half]
        rows = pl.ds(chunk * group, group)
        cols = pl.ds(half * rank, rank)
        if stage == 0:
            source = part_ref.at[rows, 3 - my_head, :, cols]
        elif stage == 1:
            source = part_ref.at[rows, target, :, cols]
        else:
            source, target = passed_ref.at[rows, :, cols], other
        return pltpu.make_async_remote_copy(
            src_ref=source,
            dst_ref=landed_ref.at[stage, rows, :, cols],
            send_sem=sum_send.at[chunk, 2 * stage + half],
            recv_sem=sum_recv.at[chunk, 2 * stage + half],
            device_id=(my_ctx, target),
            device_id_type=pl.DeviceIdType.MESH,
        )

    def pass_on(chunk):
        rows = pl.ds(chunk * group, group)
        near = (my_head + 1 - 2 * lax.rem(my_head, 2), lax.rem(my_head + 2, 4))
        for half in range(2):
            cols = slice(half * rank, (half + 1) * rank)
            pair_copy(chunk, 0, half).wait_recv()
            passed_ref[rows, :, cols] = (
                part_ref[rows, near[1 - half], :, cols].astype(jnp.float32)
                + landed_ref[0, rows, :, cols].astype(jnp.float32)
            ).astype(jnp.bfloat16)
            pair_copy(chunk, 2, half).start()

    def move_copy(step):
        return pltpu.make_async_remote_copy(
            src_ref=share_ref.at[step],
            dst_ref=moved_ref.at[step],
            send_sem=move_send.at[step],
            recv_sem=move_recv.at[step],
            device_id=(ctx_of(1 + step), my_head),
            device_id_type=pl.DeviceIdType.MESH,
        )

    def gather_copy(chunk, shift):
        block = hidden_ref.at[pl.ds(chunk * group, group), my_head]
        return pltpu.make_async_remote_copy(
            src_ref=block,
            dst_ref=block,
            send_sem=gather_send.at[chunk, shift - 1],
            recv_sem=gather_recv.at[chunk, shift - 1],
            device_id=(my_ctx, head_of(shift)),
            device_id_type=pl.DeviceIdType.MESH,
        )

    def summed(chunk):
        rows = pl.ds(chunk * group, group)
        if square:
            total = part_ref[rows, my_head].astype(jnp.float32)
            for stage in (1, 2):
                for half in range(2):
                    pair_copy(chunk, stage, half).wait_recv()
                total = total + landed_ref[stage, rows].astype(jnp.float32)
            return total
        for shift in range(1, head_size):
            sum_copy(chunk, shift).wait_recv()
        total = part_ref[rows, my_head].astype(jnp.float32)
        for shift in range(1, head_size):
            total = total + landed_ref[shift - 1, rows].astype(jnp.float32)
        return total

    w_copy(0).start()
    for step in range(ctx_size):
        for member in range(2):
            x_copy(member, step).start()
        if step == group - 1:
            w_copy(1).start()
    for slab in range(2, 4):
        w_copy(slab).start()
    for step in range(ctx_size):
        for member in range(2):
            y_copy(member, step).start()

    barrier = pltpu.get_barrier_semaphore()
    for shift in range(1, head_size):
        pl.semaphore_signal(
            barrier,
            inc=1,
            device_id=(my_ctx, head_of(shift)),
            device_id_type=pl.DeviceIdType.MESH,
        )
    for shift in range(1, ctx_size):
        pl.semaphore_signal(
            barrier,
            inc=1,
            device_id=(ctx_of(shift), my_head),
            device_id_type=pl.DeviceIdType.MESH,
        )
    pl.semaphore_wait(barrier, head_size - 1 + ctx_size - 1)

    def project(chunk, _):
        side = chunk // chunks

        @pl.when(lax.rem(chunk, chunks) == 0)
        def _():
            for member in range(2):
                slab = 2 * side + member
                pltpu.make_async_copy(w_hbm.at[0], packed_ref.at[slab], w_sem.at[slab]).wait()

                def split(part, _):
                    pairs = flat_ref[slab, pl.ds(part * 2 * w_rows, 2 * w_rows), :]
                    halves = pltpu.einshape("(kh)l->hkl", pairs, h=2)
                    band = pl.ds(part * w_rows, w_rows)
                    for half in range(2):
                        w_ref[member, half, band, :] = halves[half]
                    return 0

                lax.fori_loop(0, width // w_rows, split, 0)

        for extra in range(group):
            for member in range(2):
                step = chunk * group + extra
                pltpu.make_async_copy(
                    recv_k_ref.at[0], x_ref.at[member, step], x_sem.at[member, step]
                ).wait()
        rows = pl.ds(chunk * group, group)
        for half in range(2):
            total = None
            for member in range(2):
                term = jnp.dot(
                    x_ref[member, rows].reshape(group * block_rows, width),
                    w_ref[member, half],
                    preferred_element_type=jnp.float32,
                )
                total = term if total is None else total + term
            part_ref[rows, :, :, half * rank : (half + 1) * rank] = total.astype(
                jnp.bfloat16
            ).reshape(group, head_size, sub, rank)
        if square:
            for stage in range(2):
                for half in range(2):
                    pair_copy(chunk, stage, half).start()

            @pl.when(chunk >= 1)
            def _():
                pass_on(chunk - 1)
        else:
            for shift in range(1, head_size):
                sum_copy(chunk, shift).start()

        @pl.when(chunk >= chunks)
        def _():
            first = chunk - chunks
            total = summed(first).astype(jnp.bfloat16)
            share_ref[pl.ds(first * group, group)] = total

            for extra in range(group):
                step = first * group + extra

                @pl.when(step < ctx_size - 1)
                def _():
                    move_copy(step).start()

        return 0

    lax.fori_loop(0, 2 * chunks, project, 0)
    if square:
        pass_on(2 * chunks - 1)

    def finish(chunk, _):
        total = summed(chunk + chunks)
        for extra in range(group):
            step = chunk * group + extra

            @pl.when(step < ctx_size - 1)
            def _():
                move_copy(step).wait_recv()

            @pl.when(step == ctx_size - 1)
            def _():
                moved_ref[ctx_size - 1] = share_ref[ctx_size - 1]

        rows = pl.ds(chunk * group, group)
        total = total + moved_ref[rows].astype(jnp.float32)
        gate, up = total[..., :rank], total[..., rank:]
        hidden_ref[rows, my_head] = (gate / (1.0 + jnp.exp(-gate)) * up).astype(jnp.bfloat16)
        for shift in range(1, head_size):
            gather_copy(chunk, shift).start()
        return 0

    lax.fori_loop(0, chunks, finish, 0)

    def out_copy(step):
        return pltpu.make_async_copy(
            hidden_ref.at[step], out_ref.at[ctx_of(-1 - step)], out_sem.at[step]
        )

    def deliver(chunk, _):
        for shift in range(1, head_size):
            source = head_of(head_size - shift)
            block = hidden_ref.at[pl.ds(chunk * group, group), source]
            pltpu.make_async_remote_copy(
                src_ref=block,
                dst_ref=block,
                send_sem=gather_send.at[chunk, shift - 1],
                recv_sem=gather_recv.at[chunk, shift - 1],
                device_id=(my_ctx, head_of(shift)),
                device_id_type=pl.DeviceIdType.MESH,
            ).wait_recv()
        for extra in range(group):
            out_copy(chunk * group + extra).start()
        return 0

    lax.fori_loop(0, chunks, deliver, 0)

    def drain(chunk, _):
        if square:
            for stage in range(3):
                for half in range(2):
                    pair_copy(chunk, stage, half).wait_send()
                    pair_copy(chunk + chunks, stage, half).wait_send()
        for shift in range(1, head_size):
            if not square:
                sum_copy(chunk, shift).wait_send()
                sum_copy(chunk + chunks, shift).wait_send()
            gather_copy(chunk, shift).wait_send()
        for extra in range(group):
            step = chunk * group + extra

            @pl.when(step < ctx_size - 1)
            def _():
                move_copy(step).wait_send()

            out_copy(step).wait()
        return 0

    lax.fori_loop(0, chunks, drain, 0)


def exchange(sharer_k, sharer_v, recv_k, recv_v, weights, ctx_size, head_size):
    _, block_rows, width = sharer_k.shape
    rank = weights.shape[-1]
    sub = block_rows // head_size
    chunks = math.gcd(ctx_size, 4)
    blocks = (ctx_size, block_rows, width)
    anywhere = pl.BlockSpec(memory_space=pl.ANY)
    dma = pltpu.SemaphoreType.DMA
    bf16 = jnp.bfloat16
    return pl.pallas_call(
        functools.partial(
            exchange_kernel, ctx_size=ctx_size, head_size=head_size, chunks=chunks
        ),
        in_specs=[anywhere] * 5,
        out_specs=anywhere,
        out_shape=jax.ShapeDtypeStruct((ctx_size, head_size, sub, rank), bf16),
        scratch_shapes=[
            pltpu.VMEM((2, 2 * ctx_size, block_rows, width), bf16),
            pltpu.VMEM((4, width, 2, rank), bf16),
            pltpu.VMEM((2, 2, width, rank), bf16),
            pltpu.VMEM((2 * ctx_size, head_size, sub, 2 * rank), bf16),
            pltpu.VMEM((head_size - 1, 2 * ctx_size, sub, 2 * rank), bf16),
            pltpu.VMEM((2 * ctx_size, sub, 2 * rank), bf16),
            pltpu.VMEM((ctx_size, sub, 2 * rank), bf16),
            pltpu.VMEM((ctx_size, sub, 2 * rank), bf16),
            pltpu.VMEM((ctx_size, head_size, sub, rank), bf16),
            dma((2, 2 * ctx_size)),
            dma((4,)),
            dma((2 * chunks, max(6, head_size - 1))),
            dma((2 * chunks, max(6, head_size - 1))),
            dma((ctx_size,)),
            dma((ctx_size,)),
            dma((chunks, head_size - 1)),
            dma((chunks, head_size - 1)),
            dma((ctx_size,)),
        ],
        compiler_params=pltpu.CompilerParams(
            collective_id=0, has_side_effects=True, vmem_limit_bytes=60 * 1024 * 1024
        ),
        name="exchange",
    )(sharer_k, sharer_v, recv_k.reshape(blocks), recv_v.reshape(blocks), weights)


def near_exchange_kernel(
    sharer_k_ref,
    sharer_v_ref,
    recv_k_ref,
    recv_v_ref,
    w_hbm,
    out_ref,
    x_ref,
    packed_ref,
    w_ref,
    part_ref,
    landed_ref,
    passed_ref,
    share_ref,
    moved_ref,
    hidden_ref,
    raw_ref,
    x_sem,
    w_sem,
    sum_send,
    sum_recv,
    raw_send,
    raw_recv,
    move_send,
    move_recv,
    gather_send,
    gather_recv,
    out_sem,
    *,
    ctx_size,
    head_size,
):
    my_ctx = lax.axis_index("ctx")
    my_head = lax.axis_index("heads")
    group = 2
    chunks = ctx_size // group
    far = ctx_size - 4
    far_chunks = far // group
    hoods = ctx_size // 4
    hood = my_ctx // 4
    seat = lax.rem(my_ctx, 4)
    near = (my_head + 1 - 2 * lax.rem(my_head, 2), lax.rem(my_head + 2, 4))
    block_rows, width = x_ref.shape[2:]
    rank = w_ref.shape[-1]
    sub = block_rows // head_size
    w_rows = math.gcd(width, 128)
    flat_ref = packed_ref.reshape(4, 2 * width, rank)

    def ctx_of(shift):
        return lax.rem(my_ctx + shift, ctx_size)

    def target_of(step):
        other = lax.rem(hood + 1 + step // 4, hoods)
        return other * 4 + lax.rem(seat + lax.rem(step + 2, 4), 4)

    def source_of(step):
        other = lax.rem(hood + 2 * hoods - 1 - step // 4, hoods)
        return other * 4 + lax.rem(seat + 4 - lax.rem(step + 2, 4), 4)

    def head_of(shift):
        return lax.rem(my_head + shift, head_size)

    def x_copy(member, step):
        sharer = (sharer_k_ref, sharer_v_ref)[member]
        return pltpu.make_async_copy(
            sharer.at[target_of(step)], x_ref.at[member, step], x_sem.at[member, step]
        )

    def y_copy(member, step):
        recv = (recv_k_ref, recv_v_ref)[member]
        return pltpu.make_async_copy(
            recv.at[source_of(step)],
            x_ref.at[member, ctx_size + step],
            x_sem.at[member, ctx_size + step],
        )

    def w_copy(slab):
        return pltpu.make_async_copy(w_hbm.at[slab], packed_ref.at[slab], w_sem.at[slab])

    def pair_copy(chunk, stage, half):
        target, other = near[half], near[1 - half]
        rows = pl.ds(chunk * group, group)
        cols = pl.ds(half * rank, rank)
        if stage == 0:
            source = part_ref.at[rows, 3 - my_head, :, cols]
        elif stage == 1:
            source = part_ref.at[rows, target, :, cols]
        else:
            source, target = passed_ref.at[rows, :, cols], other
        return pltpu.make_async_remote_copy(
            src_ref=source,
            dst_ref=landed_ref.at[stage, rows, :, cols],
            send_sem=sum_send.at[chunk, 2 * stage + half],
            recv_sem=sum_recv.at[chunk, 2 * stage + half],
            device_id=(my_ctx, target),
            device_id_type=pl.DeviceIdType.MESH,
        )

    def pass_on(chunk):
        rows = pl.ds(chunk * group, group)
        for half in range(2):
            cols = slice(half * rank, (half + 1) * rank)
            pair_copy(chunk, 0, half).wait_recv()
            passed_ref[rows, :, cols] = (
                part_ref[rows, near[1 - half], :, cols].astype(jnp.float32)
                + landed_ref[0, rows, :, cols].astype(jnp.float32)
            ).astype(jnp.bfloat16)
            pair_copy(chunk, 2, half).start()

    def move_copy(step):
        return pltpu.make_async_remote_copy(
            src_ref=share_ref.at[step],
            dst_ref=moved_ref.at[step],
            send_sem=move_send.at[step],
            recv_sem=move_recv.at[step],
            device_id=(target_of(step), my_head),
            device_id_type=pl.DeviceIdType.MESH,
        )

    def raw_copy(step):
        return pltpu.make_async_remote_copy(
            src_ref=part_ref.at[step],
            dst_ref=raw_ref.at[step - far],
            send_sem=raw_send.at[step - far],
            recv_sem=raw_recv.at[step - far],
            device_id=(target_of(step), my_head),
            device_id_type=pl.DeviceIdType.MESH,
        )

    def gather_copy(chunk, side):
        block = hidden_ref.at[pl.ds(chunk * group, group), my_head]
        return pltpu.make_async_remote_copy(
            src_ref=block,
            dst_ref=block,
            send_sem=gather_send.at[chunk, side],
            recv_sem=gather_recv.at[chunk, side],
            device_id=(my_ctx, near[side]),
            device_id_type=pl.DeviceIdType.MESH,
        )

    def arrived_copy(chunk, side):
        block = hidden_ref.at[pl.ds(chunk * group, group), near[side]]
        return pltpu.make_async_remote_copy(
            src_ref=block,
            dst_ref=block,
            send_sem=gather_send.at[chunk, side],
            recv_sem=gather_recv.at[chunk, side],
            device_id=(my_ctx, near[side]),
            device_id_type=pl.DeviceIdType.MESH,
        )

    def relay_copy(chunk, half, owner):
        cols = pl.ds(half * (rank // 2), rank // 2)
        block = hidden_ref.at[pl.ds(chunk * group, group), owner, :, cols]
        return pltpu.make_async_remote_copy(
            src_ref=block,
            dst_ref=block,
            send_sem=gather_send.at[chunk, 2 + half],
            recv_sem=gather_recv.at[chunk, 2 + half],
            device_id=(my_ctx, near[1 - half]),
            device_id_type=pl.DeviceIdType.MESH,
        )

    def relay(chunk):
        for half in range(2):
            arrived_copy(chunk, half).wait_recv()
            relay_copy(chunk, half, near[half]).start()

    def summed(chunk):
        rows = pl.ds(chunk * group, group)
        total = part_ref[rows, my_head].astype(jnp.float32)
        for stage in (1, 2):
            for half in range(2):
                pair_copy(chunk, stage, half).wait_recv()
            total = total + landed_ref[stage, rows].astype(jnp.float32)
        return total

    w_copy(0).start()
    for step in range(ctx_size):
        for member in range(2):
            x_copy(member, step).start()
        if step == group - 1:
            w_copy(1).start()
    for slab in range(2, 4):
        w_copy(slab).start()
    for step in range(ctx_size):
        for member in range(2):
            y_copy(member, step).start()

    barrier = pltpu.get_barrier_semaphore()
    for shift in range(1, head_size):
        pl.semaphore_signal(
            barrier,
            inc=1,
            device_id=(my_ctx, head_of(shift)),
            device_id_type=pl.DeviceIdType.MESH,
        )
    for shift in range(1, ctx_size):
        pl.semaphore_signal(
            barrier,
            inc=1,
            device_id=(ctx_of(shift), my_head),
            device_id_type=pl.DeviceIdType.MESH,
        )
    pl.semaphore_wait(barrier, head_size - 1 + ctx_size - 1)

    def project(chunk, _):
        side = chunk // chunks

        @pl.when(lax.rem(chunk, chunks) == 0)
        def _():
            for member in range(2):
                slab = 2 * side + member
                pltpu.make_async_copy(w_hbm.at[0], packed_ref.at[slab], w_sem.at[slab]).wait()

                def split(part, _):
                    pairs = flat_ref[slab, pl.ds(part * 2 * w_rows, 2 * w_rows), :]
                    halves = pltpu.einshape("(kh)l->hkl", pairs, h=2)
                    band = pl.ds(part * w_rows, w_rows)
                    for half in range(2):
                        w_ref[member, half, band, :] = halves[half]
                    return 0

                lax.fori_loop(0, width // w_rows, split, 0)

        for extra in range(group):
            for member in range(2):
                step = chunk * group + extra
                pltpu.make_async_copy(
                    recv_k_ref.at[0], x_ref.at[member, step], x_sem.at[member, step]
                ).wait()
        rows = pl.ds(chunk * group, group)
        for half in range(2):
            total = None
            for member in range(2):
                term = jnp.dot(
                    x_ref[member, rows].reshape(group * block_rows, width),
                    w_ref[member, half],
                    preferred_element_type=jnp.float32,
                )
                total = term if total is None else total + term
            part_ref[rows, :, :, half * rank : (half + 1) * rank] = total.astype(
                jnp.bfloat16
            ).reshape(group, head_size, sub, rank)
        @pl.when(chunk >= 2 * chunks - 2)
        def _():
            for extra in range(group):
                step = (chunk - chunks) * group + extra
                slot = ctx_size + step

                def add(other):
                    part_ref[slot] = (
                        part_ref[slot].astype(jnp.float32) + other.astype(jnp.float32)
                    ).astype(jnp.bfloat16)

                @pl.when(step == ctx_size - 2)
                def _():
                    add(part_ref[ctx_size - 2])

                @pl.when(step != ctx_size - 2)
                def _():
                    raw_copy(step).wait_recv()
                    add(raw_ref[step - far])

        is_near = jnp.logical_and(chunk >= far_chunks, chunk < chunks)

        @pl.when(jnp.logical_not(is_near))
        def _():
            for stage in range(2):
                for half in range(2):
                    pair_copy(chunk, stage, half).start()

        @pl.when(is_near)
        def _():
            for extra in range(group):
                step = chunk * group + extra

                @pl.when(step != ctx_size - 2)
                def _():
                    raw_copy(step).start()

        last = chunk - 1

        @pl.when(
            jnp.logical_or(jnp.logical_and(last >= 0, last < far_chunks), last >= chunks)
        )
        def _():
            pass_on(last)

        @pl.when(jnp.logical_and(chunk >= chunks, chunk < chunks + far_chunks))
        def _():
            first = chunk - chunks
            total = summed(first).astype(jnp.bfloat16)
            share_ref[pl.ds(first * group, group)] = total
            for extra in range(group):
                move_copy(first * group + extra).start()

        return 0

    lax.fori_loop(0, 2 * chunks, project, 0)
    pass_on(2 * chunks - 1)

    def activate(chunk, total):
        gate, up = total[..., :rank], total[..., rank:]
        hidden_ref[pl.ds(chunk * group, group), my_head] = (
            gate / (1.0 + jnp.exp(-gate)) * up
        ).astype(jnp.bfloat16)
        for side in range(2):
            gather_copy(chunk, side).start()

    def finish(chunk, _):
        total = summed(chunk + chunks)

        @pl.when(chunk < far_chunks)
        def _():
            for extra in range(group):
                move_copy(chunk * group + extra).wait_recv()
            moved = moved_ref[pl.ds(chunk * group, group)].astype(jnp.float32)
            activate(chunk, total + moved)

        @pl.when(chunk >= far_chunks)
        def _():
            activate(chunk, total)

        @pl.when(chunk >= 1)
        def _():
            relay(chunk - 1)

        return 0

    lax.fori_loop(0, chunks, finish, 0)
    relay(chunks - 1)

    def out_copy(step):
        return pltpu.make_async_copy(
            hidden_ref.at[step], out_ref.at[source_of(step)], out_sem.at[step]
        )

    def deliver(chunk, _):
        for half in range(2):
            relay_copy(chunk, half, 3 - my_head).wait_recv()
        for extra in range(group):
            out_copy(chunk * group + extra).start()
        return 0

    lax.fori_loop(0, chunks, deliver, 0)

    def drain(chunk, _):
        for stage in range(3):
            for half in range(2):
                pair_copy(chunk + chunks, stage, half).wait_send()

        @pl.when(chunk < far_chunks)
        def _():
            for stage in range(3):
                for half in range(2):
                    pair_copy(chunk, stage, half).wait_send()
            for extra in range(group):
                move_copy(chunk * group + extra).wait_send()

        for half in range(2):
            gather_copy(chunk, half).wait_send()
            relay_copy(chunk, half, near[half]).wait_send()
        for extra in range(group):
            step = chunk * group + extra

            @pl.when(jnp.logical_and(step >= far, step != ctx_size - 2))
            def _():
                raw_copy(step).wait_send()

            out_copy(step).wait()
        return 0

    lax.fori_loop(0, chunks, drain, 0)


def near_exchange(sharer_k, sharer_v, recv_k, recv_v, weights, ctx_size, head_size):
    _, block_rows, width = sharer_k.shape
    rank = weights.shape[-1]
    sub = block_rows // head_size
    chunks = ctx_size // 2
    blocks = (ctx_size, block_rows, width)
    anywhere = pl.BlockSpec(memory_space=pl.ANY)
    dma = pltpu.SemaphoreType.DMA
    bf16 = jnp.bfloat16
    return pl.pallas_call(
        functools.partial(near_exchange_kernel, ctx_size=ctx_size, head_size=head_size),
        in_specs=[anywhere] * 5,
        out_specs=anywhere,
        out_shape=jax.ShapeDtypeStruct((ctx_size, head_size, sub, rank), bf16),
        scratch_shapes=[
            pltpu.VMEM((2, 2 * ctx_size, block_rows, width), bf16),
            pltpu.VMEM((4, width, 2, rank), bf16),
            pltpu.VMEM((2, 2, width, rank), bf16),
            pltpu.VMEM((2 * ctx_size, head_size, sub, 2 * rank), bf16),
            pltpu.VMEM((head_size - 1, 2 * ctx_size, sub, 2 * rank), bf16),
            pltpu.VMEM((2 * ctx_size, sub, 2 * rank), bf16),
            pltpu.VMEM((ctx_size, sub, 2 * rank), bf16),
            pltpu.VMEM((ctx_size, sub, 2 * rank), bf16),
            pltpu.VMEM((ctx_size, head_size, sub, rank), bf16),
            pltpu.VMEM((4, head_size, sub, 2 * rank), bf16),
            dma((2, 2 * ctx_size)),
            dma((4,)),
            dma((2 * chunks, 6)),
            dma((2 * chunks, 6)),
            dma((4,)),
            dma((4,)),
            dma((ctx_size,)),
            dma((ctx_size,)),
            dma((chunks, 4)),
            dma((chunks, 4)),
            dma((ctx_size,)),
        ],
        compiler_params=pltpu.CompilerParams(
            collective_id=1, has_side_effects=True, vmem_limit_bytes=60 * 1024 * 1024
        ),
        name="near_exchange",
    )(sharer_k, sharer_v, recv_k.reshape(blocks), recv_v.reshape(blocks), weights)


def local(
    sharer_k,
    sharer_v,
    recv_k,
    recv_v,
    mixer_in,
    mixer_out,
    mixer_gain,
    queries,
    suffix_k,
    suffix_v,
    suffix_len,
    cache_offset,
):
    requests, ctx_total, width = recv_k.shape
    rank = mixer_in.shape[3]
    ctx_size, head_size = lax.axis_size("ctx"), lax.axis_size("heads")
    paired = head_size == 4 and ctx_size % 8 == 0
    hidden = (near_exchange if paired else exchange)(
        sharer_k, sharer_v, recv_k, recv_v, mixer_in, ctx_size, head_size
    )
    hidden = hidden.reshape(requests, ctx_total, rank)
    return tuple(
        merge_attend(
            hidden,
            mixer_out,
            mixer_gain,
            recv_k,
            recv_v,
            queries,
            suffix_k,
            suffix_v,
            suffix_len,
            cache_offset,
        )
    )


def solution(mesh):
    cache = P("ctx", None, "heads")
    placed = (
        P(None, "ctx", "heads"),
        P(None, "ctx", "heads"),
        cache,
        cache,
        P(None, "heads", None, None),
        P(None, None, "heads"),
        P(None, "heads"),
        cache,
        cache,
        cache,
        P("ctx"),
        P("ctx"),
    )
    return jax.shard_map(
        local, mesh=mesh, in_specs=placed, out_specs=(cache, cache, cache), check_vma=False
    )
```
